32 devices in a mesh: section: 2 (over core), dp: 4 (over z), mp: 4 (over y, x).
Axes of the slice: x: 2, y: 2, z: 4, core: 2. Of those that a mesh axis runs over, the one named last changes fastest.
Arguments:
- states: bfloat16 [2, 512, 4096], P('section', 'dp'), may hold values from -6 to 6
- gains: float32 [2, 4096], P('section'), may hold values from 0.25 to 1.75
- proj_a: bfloat16 [2, 4096, 4096], P('section', None, 'mp'), may hold values from -0.03125 to 0.03125
- proj_b: bfloat16 [2, 4096, 4096], P('section', None, 'mp'), may hold values from -0.09375 to 0.09375
- cotangent: bfloat16 [512, 4096], P('dp'), may hold values from -12 to 12
- src_len: int32 [4, 16], replicated, may hold values from 1 to 16, 128 in all within a row
- tgt_len: int32 [4, 16], replicated, may hold values from 1 to 16, 128 in all within a row
- dest: int32 [4, 16], replicated, may hold values from 0 to 63, as said below
Outputs:
- grad_states: bfloat16 [2, 512, 4096], P('section', 'dp')
- grad_a: float32 [2, 4096, 4096], P('section', 'dp', 'mp')
- grad_b: float32 [2, 4096, 4096], P('section', 'dp', 'mp')
The draws below stay inside these ranges and needn't reach their ends.
Inputs may be any that keep to these rules, and one draw needn't show every extreme that they name: `src_len`: each row sums to 128. `tgt_len`: each row sums to 128. `dest`: every value from 0 to 63 appears once; each row holds exactly 4 values in each range d * 16 to (d + 1) * 16 - 1.
All inputs are finite; a program needn't handle non-finite values.
Results may differ from the reference program's by a relative error of at most 0.014.
Values may be sent and summed in bfloat16 or wider, within the bound.
A program may use at most 128 MiB of HBM per device.

```python
import math
import jax
import jax.numpy as jnp
import numpy as np
from jax import lax

D = 4096
HEAD_DIM = 64
TOK_DEV = 128
SEQ_DEV = 16
INNER = 4096
MAXLEN = 16
ROWS = 512
N_DP = 4


def draw_dest(key, part):
    group = SEQ_DEV // N_DP
    send_key, slot_key = jax.random.split(jax.random.fold_in(key, 17))
    send_perm = jax.vmap(lambda one: jax.random.permutation(one, SEQ_DEV))(jax.random.split(send_key, N_DP)).astype(jnp.int32)
    slot_perm = jax.vmap(lambda one: jax.random.permutation(one, SEQ_DEV))(jax.random.split(slot_key, N_DP)).astype(jnp.int32)
    source = jnp.arange(N_DP, dtype=jnp.int32)[:, None]
    place = jnp.arange(SEQ_DEV, dtype=jnp.int32)[None, :]
    target = place // group
    slot = slot_perm[target, source * group + place % group]
    value = (target * SEQ_DEV + slot).astype(jnp.int32)
    sources = jnp.broadcast_to(source, (N_DP, SEQ_DEV))
    return jnp.zeros((N_DP, SEQ_DEV), jnp.int32).at[sources, send_perm].set(value)


def strengthened(drawn, own_key, source, target, blocks, factor):
    def block_of(position):
        return (jnp.arange(drawn.shape[position]) // (drawn.shape[position] // blocks)).reshape((-1,) + (1,) * (drawn.ndim - 1 - position))

    near = jax.random.permutation(own_key, blocks)[block_of(target)]
    second = (block_of(target) + blocks // 2) % blocks
    return jnp.where((block_of(source) == near) | (block_of(source) == second), factor * drawn, drawn)


def shard_levels(key, extent, cuts, least, high):
    loudness, own = 1.0, jax.random.fold_in(key, 6)
    for axis_at, shards_of in cuts:
        draws = jnp.exp(jax.random.uniform(jax.random.fold_in(own, axis_at), (shards_of,), jnp.float32, least / len(cuts), high / len(cuts)))
        loudness = loudness * jnp.repeat(draws, extent[axis_at] // shards_of).reshape([-1 if axis == axis_at else 1 for axis in range(len(extent))])
    return loudness


def split_up(number_of, total, limit, slope):
    weights = [(1 << 20) // math.isqrt(grade ** slope) + 1 for grade in range(2, number_of + 1)]
    spare, given = total - limit - (number_of - 1), [1] * (number_of - 1)
    while spare > 0:
        free = [i for i in range(number_of - 1) if given[i] < limit]
        pool, budget = sum([weights[i] for i in free]), spare
        for i in free:
            more = min(limit - given[i], max(1, budget * weights[i] // pool), spare)
            given[i] = given[i] + more
            spare = spare - more
    return np.array([limit] + given)


def uneven_parts(key, count, total, reach, lean):
    if count == 2:
        one = jax.random.randint(key, (), max(1, total - reach), min(reach, total - 1) + 1)
        return jnp.stack([one, total - one])
    sizes = jnp.asarray(split_up(count, total, reach, lean), jnp.int32)
    pairs = (count - 1) // 2
    donor, taker = sizes[1:1 + 2 * pairs:2], sizes[2:2 + 2 * pairs:2]
    room = jnp.minimum(donor - 1, reach - taker)
    passed = jax.random.randint(jax.random.fold_in(key, 1), (pairs,), 0, 1 << 20) % (room + 1)
    sizes = sizes.at[1:1 + 2 * pairs:2].set(donor - passed).at[2:2 + 2 * pairs:2].set(taker + passed)
    return sizes[jax.random.permutation(jax.random.fold_in(key, 2), count)]


def gaussian(stream_key, extent, spread, reach, shards=(), held_as=jnp.bfloat16):
    array = jax.random.normal(stream_key, extent, jnp.float32) * spread
    if len(shards) > 0:
        array = shard_levels(stream_key, extent, shards, -0.22, 0.18) * array
    return jnp.clip(array, min=-reach, max=reach).astype(held_as)


def heavy_noise(key, shape, deviation, limit, shards, heavy, kind=jnp.bfloat16):
    drawn = deviation * jax.random.normal(key, shape, jnp.float32)
    if shards:
        drawn = drawn * shard_levels(key, shape, shards, -0.22, 0.18)
    return jnp.clip(strengthened(drawn, jax.random.fold_in(key, 3), *heavy), -limit, limit).astype(kind)


def setup_inputs(seed: int = 0) -> dict:
    key_of = jax.random.split(jax.random.key(seed), 9)
    states = heavy_noise(key_of[0], (2, ROWS, D), 1.0, 6.0, ((0, 2), (1, 4)), (1, 2, 4, 2.0))
    gains = jnp.clip(1.0 + 0.15 * jax.random.normal(key_of[1], (2, D), jnp.float32), 0.25, 1.75)
    proj_a = gaussian(key_of[2], (2, D, INNER), (8 * D) ** -0.5, 0.03125, ((0, 2), (2, 4)))
    proj_b = gaussian(key_of[3], (2, D, INNER), D ** -0.5, 0.09375, ((0, 2), (2, 4)))
    cotangent = gaussian(key_of[4], (ROWS, D), 2.0, 12.0, ((0, 4),))
    src_len = jax.vmap(lambda own: uneven_parts(own, SEQ_DEV, TOK_DEV, MAXLEN, 2))(jax.random.split(key_of[5], N_DP)).reshape((N_DP, SEQ_DEV)).astype(jnp.int32)
    tgt_len = jax.vmap(lambda own: uneven_parts(own, SEQ_DEV, TOK_DEV, MAXLEN, 2))(jax.random.split(key_of[6], N_DP)).reshape((N_DP, SEQ_DEV)).astype(jnp.int32)
    dest = draw_dest(jax.random.fold_in(key_of[8], 71), 0)
    return {"states": states, "gains": gains, "proj_a": proj_a, "proj_b": proj_b, "cotangent": cotangent, "src_len": src_len, "tgt_len": tgt_len, "dest": dest}


EPS = 1e-06

def rms_forward(states_row, gain):
    xf = states_row.astype(jnp.float32)
    scale = lax.rsqrt(lax.optimization_barrier(jnp.mean(xf * xf, axis=-1, keepdims=True)) + EPS)
    return (xf, scale, (xf * scale * gain).astype(jnp.bfloat16))

def rms_backward(xf, scale, gain, dnorm):
    upper = gain * dnorm
    inner = lax.optimization_barrier(jnp.mean(xf * upper, axis=-1, keepdims=True))
    return (scale * upper - xf * scale * scale * scale * inner).astype(jnp.bfloat16)

def starts_of(lengths):
    count = lengths.shape[0]
    local = (jnp.cumsum(lengths, axis=1) - lengths).astype(jnp.int32)
    base = (jnp.arange(count, dtype=jnp.int32) * TOK_DEV)[:, None]
    return ((base + local).reshape(-1).astype(jnp.int32), lengths.reshape(-1).astype(jnp.int32))

def pack(rows, starts, lengths):
    steps = jnp.arange(MAXLEN, dtype=jnp.int32)
    index = starts[:, None] + steps[None, :]
    valid = steps[None, :] < lengths[:, None]
    picked = rows[jnp.minimum(index, rows.shape[0] - 1)]
    return jnp.where(valid[:, :, None], picked, jnp.zeros((), rows.dtype))

def unpack(padded, lengths):
    count, per = lengths.shape
    local = (jnp.cumsum(lengths, axis=1) - lengths).astype(jnp.int32)
    ends = local + lengths
    place = jnp.arange(TOK_DEV, dtype=jnp.int32)
    which = lax.optimization_barrier(jnp.sum((place[None, :, None] >= ends[:, None, :]).astype(jnp.int32), axis=-1)).astype(jnp.int32)
    offset = jnp.take_along_axis(local, which, axis=1)
    device = jnp.arange(count, dtype=jnp.int32)[:, None]
    flat = ((device * per + which) * MAXLEN + place[None, :] - offset).reshape(-1)
    return padded.reshape(-1, padded.shape[-1])[flat]

def attend(own, remote, key_len):
    seqs, length, width = own.shape
    cols = width // 2
    heads = cols // HEAD_DIM
    query = own[..., :cols].reshape(seqs, length, heads, HEAD_DIM)
    dout = own[..., cols:].reshape(seqs, length, heads, HEAD_DIM)
    keys = remote[..., :cols].reshape(seqs, length, heads, HEAD_DIM)
    values = remote[..., cols:].reshape(seqs, length, heads, HEAD_DIM)
    qf, df = (query.astype(jnp.float32), dout.astype(jnp.float32))
    kf, vf = (keys.astype(jnp.float32), values.astype(jnp.float32))
    scores = jnp.einsum('sqhd,skhd->shqk', qf, kf)
    live = jnp.arange(length, dtype=jnp.int32)[None, None, None, :] < key_len[:, None, None, None]
    expo = jnp.where(live, jnp.exp(scores), jnp.float32(0.0))
    weight = expo / lax.optimization_barrier(jnp.sum(expo, axis=-1, keepdims=True))
    weight_b = weight.astype(jnp.bfloat16)
    wbf = weight_b.astype(jnp.float32)
    attended = jnp.einsum('shqk,skhd->sqhd', wbf, vf).astype(jnp.bfloat16)
    dweight = jnp.einsum('sqhd,skhd->shqk', df, vf)
    total = lax.optimization_barrier(jnp.sum(weight * dweight, axis=-1, keepdims=True))
    dscore = (weight * (dweight - total)).astype(jnp.bfloat16).astype(jnp.float32)
    dquery = jnp.einsum('shqk,skhd->sqhd', dscore, kf).astype(jnp.bfloat16)
    dkeys = jnp.einsum('shqk,sqhd->skhd', dscore, qf).astype(jnp.bfloat16)
    dvalues = jnp.einsum('shqk,sqhd->skhd', wbf, df).astype(jnp.bfloat16)
    front = jnp.concatenate([dquery.reshape(seqs, length, cols), attended.reshape(seqs, length, cols)], axis=-1)
    back = jnp.concatenate([dkeys.reshape(seqs, length, cols), dvalues.reshape(seqs, length, cols)], axis=-1)
    return (front, back)

def left_product(left, right):
    return lax.dot_general(left, right, (((0,), (0,)), ((), ())), preferred_element_type=jnp.float32)

def right_product(rows, weight):
    return lax.dot_general(rows, weight, (((1,), (1,)), ((), ())), preferred_element_type=jnp.float32)

def reference(states, gains, proj_a, proj_b, cotangent, src_len, tgt_len, dest):
    enc_x, enc_scale, enc_norm = rms_forward(states[0], gains[0])
    dec_x, dec_scale, dec_norm = rms_forward(states[1], gains[1])
    keys = jnp.dot(enc_norm, proj_a[0], preferred_element_type=jnp.float32).astype(jnp.bfloat16)
    values = jnp.dot(enc_norm, proj_b[0], preferred_element_type=jnp.float32).astype(jnp.bfloat16)
    query = jnp.dot(dec_norm, proj_a[1], preferred_element_type=jnp.float32).astype(jnp.bfloat16)
    dout = jnp.dot(cotangent, proj_b[1], preferred_element_type=jnp.float32).astype(jnp.bfloat16)
    flat_dest = dest.reshape(-1).astype(jnp.int32)
    total = flat_dest.shape[0]
    inverse = jnp.zeros((total,), jnp.int32).at[flat_dest].set(jnp.arange(total, dtype=jnp.int32))
    src_start, src_flat = starts_of(src_len)
    tgt_start, tgt_flat = starts_of(tgt_len)
    remote = pack(jnp.concatenate([keys, values], axis=1), src_start[inverse], src_flat[inverse])
    own = pack(jnp.concatenate([query, dout], axis=1), tgt_start, tgt_flat)
    front, back = attend(own, remote, src_flat[inverse])
    dec_rows = unpack(front, tgt_len)
    enc_rows = unpack(back[flat_dest], src_len)
    cols = proj_a.shape[2]
    dquery, attended = (dec_rows[:, :cols], dec_rows[:, cols:])
    dkeys, dvalues = (enc_rows[:, :cols], enc_rows[:, cols:])
    enc_dnorm = right_product(dkeys, proj_a[0]) + right_product(dvalues, proj_b[0])
    dec_dnorm = right_product(dquery, proj_a[1])
    grad_states = jnp.stack([rms_backward(enc_x, enc_scale, gains[0], enc_dnorm), rms_backward(dec_x, dec_scale, gains[1], dec_dnorm)])
    grad_a = jnp.stack([left_product(enc_norm, dkeys), left_product(dec_norm, dquery)])
    grad_b = jnp.stack([left_product(enc_norm, dvalues), left_product(cotangent, attended)])
    return (grad_states, grad_a, grad_b)
```

```python
import functools

import jax
import jax.numpy as jnp
from jax import lax
from jax.experimental import pallas as pl
from jax.experimental.pallas import tpu as pltpu
from jax.sharding import PartitionSpec as P

HEAD_DIM = 64
LANES = 128
EPS = 1e-06
MESH = pl.DeviceIdType.MESH


def rms_forward(states_row, gain):
    xf = states_row.astype(jnp.float32)
    scale = lax.rsqrt(jnp.mean(xf * xf, axis=-1, keepdims=True) + EPS)
    return (xf, scale, (xf * scale * gain).astype(jnp.bfloat16))


def left_product(left, right):
    return lax.dot_general(
        left, right, (((0,), (0,)), ((), ())), preferred_element_type=jnp.float32
    )


def right_product(rows, weight):
    return lax.dot_general(
        rows, weight, (((1,), (1,)), ((), ())), preferred_element_type=jnp.float32
    )


def sequence_of(lengths, names, tokens):
    slot = jnp.arange(lengths.shape[1], dtype=jnp.int32)
    upto = (slot[:, None] <= slot[None, :]).astype(jnp.int32)
    ends = jnp.sum(lengths[:, :, None] * upto[None], axis=1)
    starts = ends - lengths
    place = jnp.arange(tokens, dtype=jnp.int32)
    inside = (place[None, :, None] >= starts[:, None, :]) & (
        place[None, :, None] < ends[:, None, :]
    )
    return jnp.sum(jnp.where(inside, names[:, None, :], 0), axis=-1).reshape(-1)


def exchange_kernel(
    n, m, paired, normed, second, own_all, other_all, mine_a, mine_b,
    line_send, line_recv, sec_send, sec_recv, za_send, za_recv, mp_send, mp_recv,
    loc_sem,
):
    me = lax.axis_index("dp")
    col = lax.axis_index("mp")
    sec = lax.axis_index("section")
    tokens, width = normed.shape
    part = tokens // m
    cols = width // n
    barrier = pltpu.get_barrier_semaphore()
    for j in range(1, n):
        pl.semaphore_signal(
            barrier, inc=1, device_id={"dp": lax.rem(me + j, n)}, device_id_type=MESH
        )
    for j in range(1, m):
        pl.semaphore_signal(
            barrier, inc=1, device_id={"mp": lax.rem(col + j, m)}, device_id_type=MESH
        )
    pl.semaphore_signal(barrier, inc=1, device_id={"section": 1 - sec}, device_id_type=MESH)
    pl.semaphore_wait(barrier, n + m - 1)

    band = pl.ds(pl.multiple_of(col * part, part), part)

    def line_copy(way, s):
        chunk = me - s if way == 0 else me + s
        target = me + 1 if way == 0 else me - 1
        src = paired if s == 0 else own_all.at[chunk]
        return pltpu.make_async_remote_copy(
            src_ref=src, dst_ref=own_all.at[chunk],
            send_sem=line_send.at[way, s], recv_sem=line_recv.at[way, s],
            device_id={"dp": target}, device_id_type=MESH,
        )

    def line_ok(way, s):
        if way == 0:
            return jnp.logical_and(me - s >= 0, me < n - 1)
        return jnp.logical_and(me + s <= n - 1, me > 0)

    def got(way, s):
        return me - 1 - s >= 0 if way == 0 else me + 1 + s <= n - 1

    def sec_copy(chunk, src):
        return pltpu.make_async_remote_copy(
            src_ref=src, dst_ref=other_all.at[chunk],
            send_sem=sec_send.at[chunk], recv_sem=sec_recv.at[chunk],
            device_id={"section": 1 - sec}, device_id_type=MESH,
        )

    def za_copy(which, j):
        src, dst = ((normed, mine_a), (second, mine_b))[which]
        peer = lax.rem(me + j, n)
        return pltpu.make_async_remote_copy(
            src_ref=src.at[band, pl.ds(pl.multiple_of(peer * cols, cols), cols)],
            dst_ref=dst.at[me, band, :],
            send_sem=za_send.at[which, j], recv_sem=za_recv.at[which, j],
            device_id={"dp": peer}, device_id_type=MESH,
        )

    def mp_copy(which, j):
        dst = (mine_a, mine_b)[which]
        return pltpu.make_async_remote_copy(
            src_ref=dst.at[:, band, :], dst_ref=dst.at[:, band, :],
            send_sem=mp_send.at[which, j], recv_sem=mp_recv.at[which, j],
            device_id={"mp": lax.rem(col + j, m)}, device_id_type=MESH,
        )

    def local(which):
        src, dst = ((normed, mine_a), (second, mine_b))[which]
        return pltpu.make_async_copy(
            src.at[band, pl.ds(pl.multiple_of(me * cols, cols), cols)],
            dst.at[me, band, :], loc_sem.at[which],
        )

    def second_too(fn):
        fn(0)
        pl.when(sec == 1)(lambda: fn(1))

    keep = pltpu.make_async_copy(paired, own_all.at[me], loc_sem.at[2])
    for way in (0, 1):
        pl.when(line_ok(way, 0))(lambda way=way: line_copy(way, 0).start())
    for j in range(1, n):
        second_too(lambda which: za_copy(which, j).start())
    second_too(lambda which: local(which).start())
    keep.start()
    sec_copy(me, paired).start()

    def spread(which):
        local(which).wait()
        for j in range(1, n):
            za_copy(which, j).wait_recv()
        for j in range(1, m):
            mp_copy(which, j).start()

    second_too(spread)

    for s in range(n - 1):
        for way in (0, 1):

            @pl.when(got(way, s))
            def _():
                line_copy(way, s).wait_recv()
                chunk = me - 1 - s if way == 0 else me + 1 + s
                if s + 1 < n - 1:
                    pl.when(line_ok(way, s + 1))(lambda: line_copy(way, s + 1).start())
                sec_copy(chunk, own_all.at[chunk]).start()

    keep.wait()

    def finish(which):
        for j in range(1, n):
            za_copy(which, j).wait_send()
        for j in range(1, m):
            mp_copy(which, j).wait()

    second_too(finish)
    for s in range(n - 1):
        for way in (0, 1):
            pl.when(line_ok(way, s))(lambda way=way, s=s: line_copy(way, s).wait_send())
    for c in range(n):
        sec_copy(c, own_all.at[c]).wait()


def exchange(n, m, paired, normed, second):
    tokens, width = normed.shape
    both = jax.ShapeDtypeStruct((n,) + paired.shape, jnp.bfloat16)
    mine = jax.ShapeDtypeStruct((n, tokens, width // n), jnp.bfloat16)
    dma = pltpu.SemaphoreType.DMA
    return pl.pallas_call(
        functools.partial(exchange_kernel, n, m),
        out_shape=(both, both, mine, mine),
        in_specs=[pl.BlockSpec(memory_space=pltpu.VMEM)] * 3,
        out_specs=[pl.BlockSpec(memory_space=pl.ANY)] * 4,
        scratch_shapes=[
            dma((2, n)), dma((2, n)), dma((n,)), dma((n,)),
            dma((2, n)), dma((2, n)), dma((2, m)), dma((2, m)), dma((3,)),
        ],
        compiler_params=pltpu.CompilerParams(collective_id=0, has_side_effects=True),
        name="exchange",
    )(paired, normed, second)


def attend_kernel(step, qid_col, qid_row, kid_col, kid_row, own_a, own_b, other_a, other_b,
                  out_a, out_b, acc_a, acc_b):
    encoder = lax.axis_index("section") == 0
    rows = own_a.shape[0]
    blocks = rows // step
    lane = lax.broadcasted_iota(jnp.int32, (1, LANES), 1) // HEAD_DIM
    zero = jnp.zeros((), jnp.bfloat16)

    @pl.when(encoder)
    def _():
        keys, values = own_a[...], own_b[...]
        if blocks > 1:
            acc_a[...] = jnp.zeros_like(acc_a)
            acc_b[...] = jnp.zeros_like(acc_b)

        def block(b):
            at = pl.ds(0 if blocks == 1 else pl.multiple_of(b * step, step), step)
            query, dout = other_a[at, :], other_b[at, :]
            mask = kid_col[...] == qid_row[:, at]
            dk, dv = None, None
            for h in range(LANES // HEAD_DIM):
                qh = jnp.where(lane == h, query, zero)
                dh = jnp.where(lane == h, dout, zero)
                score = right_product(keys, qh)
                expo = jnp.exp(jnp.where(mask, score, -jnp.inf))
                weight = expo * (1.0 / jnp.sum(expo, axis=0, keepdims=True))
                dweight = right_product(values, dh)
                total = jnp.sum(weight * dweight, axis=0, keepdims=True)
                dscore = (weight * (dweight - total)).astype(jnp.bfloat16)
                pk = jnp.dot(dscore, qh, preferred_element_type=jnp.float32)
                pv = jnp.dot(weight.astype(jnp.bfloat16), dh, preferred_element_type=jnp.float32)
                dk = pk if dk is None else dk + pk
                dv = pv if dv is None else dv + pv
            if blocks == 1:
                out_a[...] = dk.astype(jnp.bfloat16)
                out_b[...] = dv.astype(jnp.bfloat16)
            else:
                acc_a[...] += dk
                acc_b[...] += dv

        if blocks == 1:
            block(0)
        else:
            pl.loop(0, blocks)(block)
        if blocks > 1:
            out_a[...] = acc_a[...].astype(jnp.bfloat16)
            out_b[...] = acc_b[...].astype(jnp.bfloat16)

    @pl.when(jnp.logical_not(encoder))
    def _():
        keys, values = other_a[...], other_b[...]

        def block(b):
            at = pl.ds(0 if blocks == 1 else pl.multiple_of(b * step, step), step)
            query, dout = own_a[at, :], own_b[at, :]
            mask = qid_col[at, :] == kid_row[...]
            dq, att = None, None
            for h in range(LANES // HEAD_DIM):
                kh = jnp.where(lane == h, keys, zero)
                vh = jnp.where(lane == h, values, zero)
                score = right_product(query, kh)
                expo = jnp.exp(jnp.where(mask, score, -jnp.inf))
                weight = expo * (1.0 / jnp.sum(expo, axis=1, keepdims=True))
                dweight = right_product(dout, vh)
                total = jnp.sum(weight * dweight, axis=1, keepdims=True)
                dscore = (weight * (dweight - total)).astype(jnp.bfloat16)
                pq = jnp.dot(dscore, kh, preferred_element_type=jnp.float32)
                pa = jnp.dot(weight.astype(jnp.bfloat16), vh, preferred_element_type=jnp.float32)
                dq = pq if dq is None else dq + pq
                att = pa if att is None else att + pa
            out_a[at, :] = dq.astype(jnp.bfloat16)
            out_b[at, :] = att.astype(jnp.bfloat16)

        if blocks == 1:
            block(0)
        else:
            pl.loop(0, blocks)(block)


def attend(qid, kid, own, other):
    rows, width = own.shape
    cols = width // 2
    steps = cols // LANES
    step = min(rows, max(LANES, (512 * 512) // rows))
    block = functools.partial(pl.BlockSpec, (rows, LANES))
    col = pl.BlockSpec((rows, 1), lambda i: (0, 0))
    row = pl.BlockSpec((1, rows), lambda i: (0, 0))
    out = jax.ShapeDtypeStruct((rows, cols), jnp.bfloat16)
    return pl.pallas_call(
        functools.partial(attend_kernel, step),
        grid=(steps,),
        out_shape=(out, out),
        in_specs=[col, row, col, row,
                  block(lambda i: (0, i)), block(lambda i: (0, i + steps)),
                  block(lambda i: (0, i)), block(lambda i: (0, i + steps))],
        out_specs=[block(lambda i: (0, i)), block(lambda i: (0, i))],
        scratch_shapes=[pltpu.VMEM((rows, LANES), jnp.float32)] * 2,
        compiler_params=pltpu.CompilerParams(vmem_limit_bytes=60 * 1024 * 1024),
        name="attend",
    )(qid[:, None], qid[None, :], kid[:, None], kid[None, :], own, own, other, other)


def reduce_kernel(m, partial, own, x_ref, gain_ref, out, landed, result, send, recv, osend, orecv, loc):
    col = lax.axis_index("mp")
    tokens = partial.shape[0]
    part = tokens // m
    barrier = pltpu.get_barrier_semaphore()
    for j in range(1, m):
        pl.semaphore_signal(
            barrier, inc=1, device_id={"mp": lax.rem(col + j, m)}, device_id_type=MESH
        )
    pl.semaphore_wait(barrier, m - 1)

    def scatter(j):
        peer = lax.rem(col + j, m)
        return pltpu.make_async_remote_copy(
            src_ref=partial.at[pl.ds(pl.multiple_of(peer * part, part), part), :],
            dst_ref=landed.at[j], send_sem=send.at[j], recv_sem=recv.at[j],
            device_id={"mp": peer}, device_id_type=MESH,
        )

    band = pl.ds(pl.multiple_of(col * part, part), part)

    def gather(j):
        return pltpu.make_async_remote_copy(
            src_ref=result, dst_ref=out.at[band, :],
            send_sem=osend.at[j], recv_sem=orecv.at[j],
            device_id={"mp": lax.rem(col + j, m)}, device_id_type=MESH,
        )

    for j in range(1, m):
        scatter(j).start()
    x = x_ref[band, :].astype(jnp.float32)
    scale = lax.rsqrt(jnp.mean(x * x, axis=-1, keepdims=True) + EPS)
    dnorm = own[...]
    for j in range(1, m):
        scatter(j).wait_recv()
        dnorm = dnorm + landed[j].astype(jnp.float32)
    upper = gain_ref[...] * dnorm
    inner = jnp.mean(x * upper, axis=-1, keepdims=True)
    result[...] = (scale * upper - x * scale * scale * scale * inner).astype(jnp.bfloat16)
    for j in range(1, m):
        gather(j).start()
    keep = pltpu.make_async_copy(result, out.at[band, :], loc)
    keep.start()
    keep.wait()
    for j in range(1, m):
        scatter(j).wait_send()
        gather(j).wait()


def reduce_norm(m, partial, own, states, gain):
    tokens, width = states.shape
    part = tokens // m
    dma = pltpu.SemaphoreType.DMA
    return pl.pallas_call(
        functools.partial(reduce_kernel, m),
        out_shape=jax.ShapeDtypeStruct((tokens, width), jnp.bfloat16),
        in_specs=[pl.BlockSpec(memory_space=pltpu.VMEM)] * 4,
        out_specs=pl.BlockSpec(memory_space=pl.ANY),
        scratch_shapes=[
            pltpu.VMEM((m, part, width), jnp.bfloat16),
            pltpu.VMEM((part, width), jnp.bfloat16),
            dma((m,)), dma((m,)), dma((m,)), dma((m,)), dma,
        ],
        compiler_params=pltpu.CompilerParams(collective_id=1, has_side_effects=True),
        name="reduce_norm",
    )(partial, own, states, gain)


def per_device(states, gains, proj_a, proj_b, cotangent, src_len, tgt_len, dest):
    encoder = lax.axis_index("section") == 0
    member = lax.axis_index("dp")
    n = lax.axis_size("dp")
    m = lax.axis_size("mp")
    gain = gains[0]
    weight_a = proj_a[0]
    weight_b = proj_b[0]
    tokens = states.shape[1]
    _, _, normed = rms_forward(states[0], gain)
    second_left = jnp.where(encoder, normed, cotangent)
    first = jnp.dot(normed, weight_a, preferred_element_type=jnp.float32).astype(jnp.bfloat16)
    second = jnp.dot(second_left, weight_b, preferred_element_type=jnp.float32).astype(jnp.bfloat16)
    paired = jnp.concatenate([first, second], axis=1)
    own, other, mine_a, mine_b = exchange(n, m, paired, normed, second_left)
    rows = n * tokens
    seqs = tgt_len.shape[1]
    names = jnp.arange(n * seqs, dtype=jnp.int32).reshape(n, seqs)
    qid = sequence_of(tgt_len, names, tokens)
    kid = sequence_of(src_len, dest, tokens)
    grad_first, grad_second = attend(
        qid, kid, own.reshape(rows, -1), other.reshape(rows, -1)
    )
    mine_a = mine_a.reshape(rows, -1)
    mine_b = jnp.where(encoder, mine_a, mine_b.reshape(rows, -1))
    own_first = lax.dynamic_slice_in_dim(grad_first, member * tokens, tokens, 0)
    own_second = lax.dynamic_slice_in_dim(grad_second, member * tokens, tokens, 0)
    own_second = jnp.where(encoder, own_second, jnp.zeros((), jnp.bfloat16))
    partial = right_product(own_first, weight_a) + right_product(own_second, weight_b)
    part = tokens // m
    mine = lax.dynamic_slice_in_dim(partial, lax.axis_index("mp") * part, part, 0)
    grad_states = reduce_norm(m, partial.astype(jnp.bfloat16), mine, states[0], gains)
    grad_a = left_product(mine_a, grad_first)
    grad_b = left_product(mine_b, grad_second)
    return (grad_states[None], grad_a[None], grad_b[None])


def solution(mesh):
    return jax.shard_map(
        per_device,
        mesh=mesh,
        in_specs=(
            P("section", "dp", None),
            P("section", None),
            P("section", None, "mp"),
            P("section", None, "mp"),
            P("dp", None),
            P(),
            P(),
            P(),
        ),
        out_specs=(P("section", "dp", None), P("section", "dp", "mp"), P("section", "dp", "mp")),
        check_vma=False,
    )
```

```python
import functools

import jax
import jax.numpy as jnp
from jax import lax
from jax.experimental import pallas as pl
from jax.experimental.pallas import tpu as pltpu
from jax.sharding import PartitionSpec as P

HEAD_DIM = 64
LANES = 128
EPS = 1e-06
MESH = pl.DeviceIdType.MESH


def rms_forward(states_row, gain):
    xf = states_row.astype(jnp.float32)
    scale = lax.rsqrt(jnp.mean(xf * xf, axis=-1, keepdims=True) + EPS)
    return (xf, scale, (xf * scale * gain).astype(jnp.bfloat16))


def left_product(left, right):
    return lax.dot_general(
        left, right, (((0,), (0,)), ((), ())), preferred_element_type=jnp.float32
    )


def right_product(rows, weight):
    return lax.dot_general(
        rows, weight, (((1,), (1,)), ((), ())), preferred_element_type=jnp.float32
    )


def sequence_of(lengths, names, tokens):
    slot = jnp.arange(lengths.shape[1], dtype=jnp.int32)
    before = slot[:, None] < slot[None, :]
    starts = jnp.sum(jnp.where(before[None], lengths[:, :, None], 0), axis=1)
    place = jnp.arange(tokens, dtype=jnp.int32)[None, :, None]
    inside = (place >= starts[:, None, :]) & (place < (starts + lengths)[:, None, :])
    return jnp.sum(jnp.where(inside, names[:, None, :], 0), axis=-1).reshape(-1)


def attend_piece(encoder, p, group, id_col, id_row, own, other, out_a, out_b, acc_a, acc_b):
    n, tokens, width = own.shape[1:]
    half = width // 2
    rows = n * tokens
    blocks = n // group
    lane = lax.broadcasted_iota(jnp.int32, (1, LANES), 1) // HEAD_DIM
    zero = jnp.zeros((), jnp.bfloat16)
    f32 = jnp.float32

    def cut(ref, which, c, at):
        lo = pl.multiple_of(which * half + c * LANES, LANES)
        return ref[p, at, :, pl.ds(lo, LANES)].reshape(-1, LANES)

    every = pl.ds(0, n)

    @pl.loop(0, half // LANES)
    def _(c):
        out_cols = pl.ds(pl.multiple_of(p * half + c * LANES, LANES), LANES)

        @pl.when(encoder)
        def _():
            keys, values = cut(own, 0, c, every), cut(own, 1, c, every)
            if blocks > 1:
                acc_a[...] = jnp.zeros_like(acc_a)
                acc_b[...] = jnp.zeros_like(acc_b)

            def block(b):
                at = pl.ds(b * group, group)
                query, dout = cut(other, 0, c, at), cut(other, 1, c, at)
                mask = id_col[...].reshape(rows, 1) == id_row[b]
                dk, dv = None, None
                for h in range(LANES // HEAD_DIM):
                    qh = jnp.where(lane == h, query, zero)
                    dh = jnp.where(lane == h, dout, zero)
                    expo = jnp.exp(jnp.where(mask, right_product(keys, qh), -jnp.inf))
                    weight = expo * (1.0 / jnp.sum(expo, axis=0, keepdims=True))
                    dweight = right_product(values, dh)
                    total = jnp.sum(weight * dweight, axis=0, keepdims=True)
                    dscore = (weight * (dweight - total)).astype(jnp.bfloat16)
                    pk = jnp.dot(dscore, qh, preferred_element_type=f32)
                    pv = jnp.dot(weight.astype(jnp.bfloat16), dh, preferred_element_type=f32)
                    dk = pk if dk is None else dk + pk
                    dv = pv if dv is None else dv + pv
                if blocks == 1:
                    out_a[:, :, out_cols] = dk.astype(jnp.bfloat16).reshape(n, tokens, LANES)
                    out_b[:, :, out_cols] = dv.astype(jnp.bfloat16).reshape(n, tokens, LANES)
                else:
                    acc_a[...] += dk
                    acc_b[...] += dv

            if blocks == 1:
                block(0)
            else:
                pl.loop(0, blocks)(block)
                out_a[:, :, out_cols] = acc_a[...].astype(jnp.bfloat16).reshape(n, tokens, LANES)
                out_b[:, :, out_cols] = acc_b[...].astype(jnp.bfloat16).reshape(n, tokens, LANES)

        @pl.when(jnp.logical_not(encoder))
        def _():
            keys, values = cut(other, 0, c, every), cut(other, 1, c, every)

            def block(b):
                at = pl.ds(b * group, group)
                query, dout = cut(own, 0, c, at), cut(own, 1, c, at)
                ids = id_col[at, :, :].reshape(group * tokens, 1)
                mask = None
                dq, att = None, None
                for h in range(LANES // HEAD_DIM):
                    kh = jnp.where(lane == h, keys, zero)
                    vh = jnp.where(lane == h, values, zero)
                    score = right_product(query, kh)
                    if mask is None:
                        span = group * tokens
                        mask = jnp.concatenate(
                            [ids == id_row[i] for i in range(rows // span)], axis=1
                        )
                    expo = jnp.exp(jnp.where(mask, score, -jnp.inf))
                    weight = expo * (1.0 / jnp.sum(expo, axis=1, keepdims=True))
                    dweight = right_product(dout, vh)
                    total = jnp.sum(weight * dweight, axis=1, keepdims=True)
                    dscore = (weight * (dweight - total)).astype(jnp.bfloat16)
                    pq = jnp.dot(dscore, kh, preferred_element_type=f32)
                    pa = jnp.dot(weight.astype(jnp.bfloat16), vh, preferred_element_type=f32)
                    dq = pq if dq is None else dq + pq
                    att = pa if att is None else att + pa
                shape = (group, tokens, LANES)
                out_a[at, :, out_cols] = dq.astype(jnp.bfloat16).reshape(shape)
                out_b[at, :, out_cols] = att.astype(jnp.bfloat16).reshape(shape)

            if blocks == 1:
                block(0)
            else:
                pl.loop(0, blocks)(block)


def forward_kernel(
    n, m, group, normed, second, id_col, id_row, proj_a, proj_b,
    out_a, out_b, mine_a, mine_b,
    wbuf, paired, own, other, acc_a, acc_b, wsem,
    line_send, line_recv, sec_send, sec_recv, za_send, za_recv, mp_send, mp_recv, loc_sem,
):
    me = lax.axis_index("dp")
    col = lax.axis_index("mp")
    sec = lax.axis_index("section")
    tokens, width = normed.shape
    pieces = wbuf.shape[1]
    half = wbuf.shape[3]
    part = tokens // m
    cols = width // n

    def weight_copy(which, p):
        src = (proj_a, proj_b)[which]
        return pltpu.make_async_copy(
            src.at[0, :, pl.ds(p * half, half)], wbuf.at[which, p], wsem.at[which, p]
        )

    for p in range(pieces):
        for which in (0, 1):
            weight_copy(which, p).start()

    barrier = pltpu.get_barrier_semaphore()
    for j in range(1, n):
        pl.semaphore_signal(
            barrier, inc=1, device_id={"dp": lax.rem(me + j, n)}, device_id_type=MESH
        )
    for j in range(1, m):
        pl.semaphore_signal(
            barrier, inc=1, device_id={"mp": lax.rem(col + j, m)}, device_id_type=MESH
        )
    pl.semaphore_signal(barrier, inc=1, device_id={"section": 1 - sec}, device_id_type=MESH)
    pl.semaphore_wait(barrier, n + m - 1)

    band = pl.ds(pl.multiple_of(col * part, part), part)

    def line_copy(way, s, p):
        chunk = me - s if way == 0 else me + s
        target = me + 1 if way == 0 else me - 1
        src = paired.at[p] if s == 0 else own.at[p, chunk]
        return pltpu.make_async_remote_copy(
            src_ref=src, dst_ref=own.at[p, chunk],
            send_sem=line_send.at[way, s, p], recv_sem=line_recv.at[way, s, p],
            device_id={"dp": target}, device_id_type=MESH,
        )

    def line_ok(way, s):
        if way == 0:
            return jnp.logical_and(me - s >= 0, me < n - 1)
        return jnp.logical_and(me + s <= n - 1, me > 0)

    def got(way, s):
        return me - 1 - s >= 0 if way == 0 else me + 1 + s <= n - 1

    def sec_copy(chunk, p, src):
        return pltpu.make_async_remote_copy(
            src_ref=src, dst_ref=other.at[p, chunk],
            send_sem=sec_send.at[chunk, p], recv_sem=sec_recv.at[chunk, p],
            device_id={"section": 1 - sec}, device_id_type=MESH,
        )

    def za_copy(which, j):
        src, dst = ((normed, mine_a), (second, mine_b))[which]
        peer = lax.rem(me + j, n)
        return pltpu.make_async_remote_copy(
            src_ref=src.at[band, pl.ds(pl.multiple_of(peer * cols, cols), cols)],
            dst_ref=dst.at[me, band, :],
            send_sem=za_send.at[which, j], recv_sem=za_recv.at[which, j],
            device_id={"dp": peer}, device_id_type=MESH,
        )

    def mp_copy(which, j):
        dst = (mine_a, mine_b)[which]
        return pltpu.make_async_remote_copy(
            src_ref=dst.at[:, band, :], dst_ref=dst.at[:, band, :],
            send_sem=mp_send.at[which, j], recv_sem=mp_recv.at[which, j],
            device_id={"mp": lax.rem(col + j, m)}, device_id_type=MESH,
        )

    def local(which):
        src, dst = ((normed, mine_a), (second, mine_b))[which]
        return pltpu.make_async_copy(
            src.at[band, pl.ds(pl.multiple_of(me * cols, cols), cols)],
            dst.at[me, band, :], loc_sem.at[which],
        )

    def keep(p):
        return pltpu.make_async_copy(paired.at[p], own.at[p, me], loc_sem.at[2 + p])

    def second_too(fn):
        fn(0)
        pl.when(sec == 1)(lambda: fn(1))

    for j in range(1, n):
        second_too(lambda which: za_copy(which, j).start())
    second_too(lambda which: local(which).start())

    for p in range(pieces):
        for which in (0, 1):
            weight_copy(which, p).wait()
            rows_in = (normed, second)[which]
            paired[p, :, which * half : (which + 1) * half] = jnp.dot(
                rows_in[...], wbuf[which, p], preferred_element_type=jnp.float32
            ).astype(jnp.bfloat16)
        for way in (0, 1):
            pl.when(line_ok(way, 0))(lambda way=way, p=p: line_copy(way, 0, p).start())
        sec_copy(me, p, paired.at[p]).start()
        keep(p).start()

    def spread(which):
        local(which).wait()
        for j in range(1, n):
            za_copy(which, j).wait_recv()
        for j in range(1, m):
            mp_copy(which, j).start()

    second_too(spread)

    for s in range(n - 1):
        for p in range(pieces):
            for way in (0, 1):

                @pl.when(got(way, s))
                def _():
                    line_copy(way, s, p).wait_recv()
                    chunk = me - 1 - s if way == 0 else me + 1 + s
                    if s + 1 < n - 1:
                        pl.when(line_ok(way, s + 1))(
                            lambda: line_copy(way, s + 1, p).start()
                        )
                    sec_copy(chunk, p, own.at[p, chunk]).start()

            if s == n - 2:
                keep(p).wait()
                for c in range(n):
                    sec_copy(c, p, own.at[p, c]).wait_recv()
                attend_piece(
                    sec == 0, p, group, id_col, id_row, own, other, out_a, out_b, acc_a, acc_b
                )

    def finish(which):
        for j in range(1, n):
            za_copy(which, j).wait_send()
        for j in range(1, m):
            mp_copy(which, j).wait()

    second_too(finish)
    for p in range(pieces):
        for s in range(n - 1):
            for way in (0, 1):
                pl.when(line_ok(way, s))(
                    lambda way=way, s=s, p=p: line_copy(way, s, p).wait_send()
                )
        for c in range(n):
            sec_copy(c, p, own.at[p, c]).wait_send()


def forward(n, m, normed, second, id_c, id_r, proj_a, proj_b):
    tokens, width = normed.shape
    inner = proj_a.shape[2]
    half = 2 * LANES
    pieces = inner // half
    rows = n * tokens
    group = max(1, min(n, 512 * 512 // (rows * tokens)))
    blocks = n // group
    grad = jax.ShapeDtypeStruct((n, tokens, inner), jnp.bfloat16)
    mine = jax.ShapeDtypeStruct((n, tokens, width // n), jnp.bfloat16)
    acc = (rows, LANES) if blocks > 1 else (8, LANES)
    dma = pltpu.SemaphoreType.DMA
    vmem = pl.BlockSpec(memory_space=pltpu.VMEM)
    anyw = pl.BlockSpec(memory_space=pl.ANY)
    bf16 = jnp.bfloat16
    return pl.pallas_call(
        functools.partial(forward_kernel, n, m, group),
        out_shape=(grad, grad, mine, mine),
        in_specs=[vmem] * 4 + [anyw] * 2,
        out_specs=[vmem, vmem, anyw, anyw],
        scratch_shapes=[
            pltpu.VMEM((2, pieces, width, half), bf16),
            pltpu.VMEM((pieces, tokens, 2 * half), bf16),
            pltpu.VMEM((pieces, n, tokens, 2 * half), bf16),
            pltpu.VMEM((pieces, n, tokens, 2 * half), bf16),
            pltpu.VMEM(acc, jnp.float32), pltpu.VMEM(acc, jnp.float32),
            dma((2, pieces)),
            dma((2, n, pieces)), dma((2, n, pieces)), dma((n, pieces)), dma((n, pieces)),
            dma((2, n)), dma((2, n)), dma((2, m)), dma((2, m)), dma((2 + pieces,)),
        ],
        compiler_params=pltpu.CompilerParams(
            collective_id=0, has_side_effects=True, vmem_limit_bytes=67000000
        ),
        name="forward",
    )(normed, second, id_c.reshape(n, tokens, 1), id_r.reshape(blocks, 1, rows // blocks),
      proj_a, proj_b)


def reduce_kernel(m, partial, own, x_ref, gain_ref, out, landed, result, send, recv, osend, orecv, loc):
    col = lax.axis_index("mp")
    tokens = partial.shape[0]
    part = tokens // m
    barrier = pltpu.get_barrier_semaphore()
    for j in range(1, m):
        pl.semaphore_signal(
            barrier, inc=1, device_id={"mp": lax.rem(col + j, m)}, device_id_type=MESH
        )
    pl.semaphore_wait(barrier, m - 1)

    def scatter(j):
        peer = lax.rem(col + j, m)
        return pltpu.make_async_remote_copy(
            src_ref=partial.at[pl.ds(pl.multiple_of(peer * part, part), part), :],
            dst_ref=landed.at[j], send_sem=send.at[j], recv_sem=recv.at[j],
            device_id={"mp": peer}, device_id_type=MESH,
        )

    band = pl.ds(pl.multiple_of(col * part, part), part)

    def gather(j):
        return pltpu.make_async_remote_copy(
            src_ref=result, dst_ref=out.at[band, :],
            send_sem=osend.at[j], recv_sem=orecv.at[j],
            device_id={"mp": lax.rem(col + j, m)}, device_id_type=MESH,
        )

    for j in range(1, m):
        scatter(j).start()
    x = x_ref[band, :].astype(jnp.float32)
    scale = lax.rsqrt(jnp.mean(x * x, axis=-1, keepdims=True) + EPS)
    dnorm = own[...]
    for j in range(1, m):
        scatter(j).wait_recv()
        dnorm = dnorm + landed[j].astype(jnp.float32)
    upper = gain_ref[...] * dnorm
    inner = jnp.mean(x * upper, axis=-1, keepdims=True)
    result[...] = (scale * upper - x * scale * scale * scale * inner).astype(jnp.bfloat16)
    for j in range(1, m):
        gather(j).start()
    keep = pltpu.make_async_copy(result, out.at[band, :], loc)
    keep.start()
    keep.wait()
    for j in range(1, m):
        scatter(j).wait_send()
        gather(j).wait()


def reduce_norm(m, partial, own, states, gain):
    tokens, width = states.shape
    part = tokens // m
    dma = pltpu.SemaphoreType.DMA
    return pl.pallas_call(
        functools.partial(reduce_kernel, m),
        out_shape=jax.ShapeDtypeStruct((tokens, width), jnp.bfloat16),
        in_specs=[pl.BlockSpec(memory_space=pltpu.VMEM)] * 4,
        out_specs=pl.BlockSpec(memory_space=pl.ANY),
        scratch_shapes=[
            pltpu.VMEM((m, part, width), jnp.bfloat16),
            pltpu.VMEM((part, width), jnp.bfloat16),
            dma((m,)), dma((m,)), dma((m,)), dma((m,)), dma,
        ],
        compiler_params=pltpu.CompilerParams(collective_id=1, has_side_effects=True),
        name="reduce_norm",
    )(partial, own, states, gain)


def per_device(states, gains, proj_a, proj_b, cotangent, src_len, tgt_len, dest):
    encoder = lax.axis_index("section") == 0
    member = lax.axis_index("dp")
    n = lax.axis_size("dp")
    m = lax.axis_size("mp")
    gain = gains[0]
    weight_a = proj_a[0]
    weight_b = proj_b[0]
    tokens = states.shape[1]
    _, _, normed = rms_forward(states[0], gain)
    second_left = jnp.where(encoder, normed, cotangent)
    rows = n * tokens
    seqs = tgt_len.shape[1]
    names = jnp.arange(n * seqs, dtype=jnp.int32).reshape(n, seqs)
    qid = sequence_of(tgt_len, names, tokens)
    kid = sequence_of(src_len, dest, tokens)
    grad_first, grad_second, mine_a, mine_b = forward(
        n, m, normed, second_left, jnp.where(encoder, kid, qid), jnp.where(encoder, qid, kid),
        proj_a, proj_b,
    )
    grad_first = grad_first.reshape(rows, -1)
    grad_second = grad_second.reshape(rows, -1)
    mine_a = mine_a.reshape(rows, -1)
    mine_b = jnp.where(encoder, mine_a, mine_b.reshape(rows, -1))
    own_first = lax.dynamic_slice_in_dim(grad_first, member * tokens, tokens, 0)
    own_second = lax.dynamic_slice_in_dim(grad_second, member * tokens, tokens, 0)
    own_second = jnp.where(encoder, own_second, jnp.zeros((), jnp.bfloat16))
    partial = right_product(own_first, weight_a) + right_product(own_second, weight_b)
    part = tokens // m
    mine = lax.dynamic_slice_in_dim(partial, lax.axis_index("mp") * part, part, 0)
    grad_states = reduce_norm(m, partial.astype(jnp.bfloat16), mine, states[0], gains)
    grad_a = left_product(mine_a, grad_first)
    grad_b = left_product(mine_b, grad_second)
    return (grad_states[None], grad_a[None], grad_b[None])


def solution(mesh):
    return jax.shard_map(
        per_device,
        mesh=mesh,
        in_specs=(
            P("section", "dp", None),
            P("section", None),
            P("section", None, "mp"),
            P("section", None, "mp"),
            P("dp", None),
            P(),
            P(),
            P(),
        ),
        out_specs=(P("section", "dp", None), P("section", "dp", "mp"), P("section", "dp", "mp")),
        check_vma=False,
    )
```

```python
import functools

import jax
import jax.numpy as jnp
from jax import lax
from jax.experimental import pallas as pl
from jax.experimental.pallas import tpu as pltpu
from jax.sharding import PartitionSpec as P

HEAD_DIM = 64
LANES = 128
EPS = 1e-06
MESH = pl.DeviceIdType.MESH


def rms_forward(states_row, gain):
    xf = states_row.astype(jnp.float32)
    scale = lax.rsqrt(jnp.mean(xf * xf, axis=-1, keepdims=True) + EPS)
    return (xf, scale, (xf * scale * gain).astype(jnp.bfloat16))


def left_product(left, right):
    return lax.dot_general(
        left, right, (((0,), (0,)), ((), ())), preferred_element_type=jnp.float32
    )


def right_product(rows, weight):
    return lax.dot_general(
        rows, weight, (((1,), (1,)), ((), ())), preferred_element_type=jnp.float32
    )


def sequence_of(lengths, names, tokens):
    slot = jnp.arange(lengths.shape[1], dtype=jnp.int32)
    before = slot[:, None] < slot[None, :]
    starts = jnp.sum(jnp.where(before[None], lengths[:, :, None], 0), axis=1)
    place = jnp.arange(tokens, dtype=jnp.int32)[None, :, None]
    inside = (place >= starts[:, None, :]) & (place < (starts + lengths)[:, None, :])
    return jnp.sum(jnp.where(inside, names[:, None, :], 0), axis=-1).reshape(-1)


def attend_piece(encoder, p, group, id_col, id_row, own, other, out_a, out_b, acc_a, acc_b):
    n, tokens, width = own.shape[1:]
    half = width // 2
    rows = n * tokens
    blocks = n // group
    lane = lax.broadcasted_iota(jnp.int32, (1, LANES), 1) // HEAD_DIM
    zero = jnp.zeros((), jnp.bfloat16)
    f32 = jnp.float32

    def cut(ref, which, c, at):
        lo = pl.multiple_of(which * half + c * LANES, LANES)
        return ref[p, at, :, pl.ds(lo, LANES)].reshape(-1, LANES)

    every = pl.ds(0, n)

    @pl.loop(0, half // LANES)
    def _(c):
        out_cols = pl.ds(pl.multiple_of(p * half + c * LANES, LANES), LANES)

        @pl.when(encoder)
        def _():
            keys, values = cut(own, 0, c, every), cut(own, 1, c, every)
            if blocks > 1:
                acc_a[...] = jnp.zeros_like(acc_a)
                acc_b[...] = jnp.zeros_like(acc_b)

            def block(b):
                at = pl.ds(b * group, group)
                query, dout = cut(other, 0, c, at), cut(other, 1, c, at)
                mask = id_col[...].reshape(rows, 1) == id_row[b]
                dk, dv = None, None
                for h in range(LANES // HEAD_DIM):
                    qh = jnp.where(lane == h, query, zero)
                    dh = jnp.where(lane == h, dout, zero)
                    expo = jnp.exp(jnp.where(mask, right_product(keys, qh), -jnp.inf))
                    weight = expo * (1.0 / jnp.sum(expo, axis=0, keepdims=True))
                    dweight = right_product(values, dh)
                    total = jnp.sum(weight * dweight, axis=0, keepdims=True)
                    dscore = (weight * (dweight - total)).astype(jnp.bfloat16)
                    pk = jnp.dot(dscore, qh, preferred_element_type=f32)
                    pv = jnp.dot(weight.astype(jnp.bfloat16), dh, preferred_element_type=f32)
                    dk = pk if dk is None else dk + pk
                    dv = pv if dv is None else dv + pv
                if blocks == 1:
                    out_a[:, :, out_cols] = dk.astype(jnp.bfloat16).reshape(n, tokens, LANES)
                    out_b[:, :, out_cols] = dv.astype(jnp.bfloat16).reshape(n, tokens, LANES)
                else:
                    acc_a[...] += dk
                    acc_b[...] += dv

            if blocks == 1:
                block(0)
            else:
                pl.loop(0, blocks)(block)
                out_a[:, :, out_cols] = acc_a[...].astype(jnp.bfloat16).reshape(n, tokens, LANES)
                out_b[:, :, out_cols] = acc_b[...].astype(jnp.bfloat16).reshape(n, tokens, LANES)

        @pl.when(jnp.logical_not(encoder))
        def _():
            keys, values = cut(other, 0, c, every), cut(other, 1, c, every)

            def block(b):
                at = pl.ds(b * group, group)
                query, dout = cut(own, 0, c, at), cut(own, 1, c, at)
                ids = id_col[at, :, :].reshape(group * tokens, 1)
                mask = None
                dq, att = None, None
                for h in range(LANES // HEAD_DIM):
                    kh = jnp.where(lane == h, keys, zero)
                    vh = jnp.where(lane == h, values, zero)
                    score = right_product(query, kh)
                    if mask is None:
                        span = group * tokens
                        mask = jnp.concatenate(
                            [ids == id_row[i] for i in range(rows // span)], axis=1
                        )
                    expo = jnp.exp(jnp.where(mask, score, -jnp.inf))
                    weight = expo * (1.0 / jnp.sum(expo, axis=1, keepdims=True))
                    dweight = right_product(dout, vh)
                    total = jnp.sum(weight * dweight, axis=1, keepdims=True)
                    dscore = (weight * (dweight - total)).astype(jnp.bfloat16)
                    pq = jnp.dot(dscore, kh, preferred_element_type=f32)
                    pa = jnp.dot(weight.astype(jnp.bfloat16), vh, preferred_element_type=f32)
                    dq = pq if dq is None else dq + pq
                    att = pa if att is None else att + pa
                shape = (group, tokens, LANES)
                out_a[at, :, out_cols] = dq.astype(jnp.bfloat16).reshape(shape)
                out_b[at, :, out_cols] = att.astype(jnp.bfloat16).reshape(shape)

            if blocks == 1:
                block(0)
            else:
                pl.loop(0, blocks)(block)


def forward_kernel(
    n, m, group, normed, second, id_col, id_row, proj_a, proj_b,
    out_a, out_b, mine_a, mine_b,
    wbuf, paired, own, other, acc_a, acc_b, wsem,
    line_send, line_recv, sec_send, sec_recv, za_send, za_recv, mp_send, mp_recv, loc_sem,
):
    me = lax.axis_index("dp")
    col = lax.axis_index("mp")
    sec = lax.axis_index("section")
    tokens, width = normed.shape
    pieces = wbuf.shape[1]
    half = wbuf.shape[3]
    part = tokens // m
    cols = width // n

    def weight_copy(which, p):
        src = (proj_a, proj_b)[which]
        return pltpu.make_async_copy(
            src.at[0, :, pl.ds(p * half, half)], wbuf.at[which, p], wsem.at[which, p]
        )

    for p in range(pieces):
        for which in (0, 1):
            weight_copy(which, p).start()

    barrier = pltpu.get_barrier_semaphore()
    for j in range(1, n):
        pl.semaphore_signal(
            barrier, inc=1, device_id={"dp": lax.rem(me + j, n)}, device_id_type=MESH
        )
    for j in range(1, m):
        pl.semaphore_signal(
            barrier, inc=1, device_id={"mp": lax.rem(col + j, m)}, device_id_type=MESH
        )
    pl.semaphore_signal(barrier, inc=1, device_id={"section": 1 - sec}, device_id_type=MESH)
    pl.semaphore_wait(barrier, n + m - 1)

    band = pl.ds(pl.multiple_of(col * part, part), part)

    def line_copy(way, s, p):
        chunk = me - s if way == 0 else me + s
        target = me + 1 if way == 0 else me - 1
        src = paired.at[p] if s == 0 else own.at[p, chunk]
        return pltpu.make_async_remote_copy(
            src_ref=src, dst_ref=own.at[p, chunk],
            send_sem=line_send.at[way, s, p], recv_sem=line_recv.at[way, s, p],
            device_id={"dp": target}, device_id_type=MESH,
        )

    def line_ok(way, s):
        if way == 0:
            return jnp.logical_and(me - s >= 0, me < n - 1)
        return jnp.logical_and(me + s <= n - 1, me > 0)

    def got(way, s):
        return me - 1 - s >= 0 if way == 0 else me + 1 + s <= n - 1

    def sec_copy(chunk, p, src):
        return pltpu.make_async_remote_copy(
            src_ref=src, dst_ref=other.at[p, chunk],
            send_sem=sec_send.at[chunk, p], recv_sem=sec_recv.at[chunk, p],
            device_id={"section": 1 - sec}, device_id_type=MESH,
        )

    def za_copy(which, j):
        src, dst = ((normed, mine_a), (second, mine_b))[which]
        peer = lax.rem(me + j, n)
        return pltpu.make_async_remote_copy(
            src_ref=src.at[band, pl.ds(pl.multiple_of(peer * cols, cols), cols)],
            dst_ref=dst.at[me, band, :],
            send_sem=za_send.at[which, j], recv_sem=za_recv.at[which, j],
            device_id={"dp": peer}, device_id_type=MESH,
        )

    def mp_copy(which, j):
        dst = (mine_a, mine_b)[which]
        return pltpu.make_async_remote_copy(
            src_ref=dst.at[:, band, :], dst_ref=dst.at[:, band, :],
            send_sem=mp_send.at[which, j], recv_sem=mp_recv.at[which, j],
            device_id={"mp": lax.rem(col + j, m)}, device_id_type=MESH,
        )

    def local(which):
        src, dst = ((normed, mine_a), (second, mine_b))[which]
        return pltpu.make_async_copy(
            src.at[band, pl.ds(pl.multiple_of(me * cols, cols), cols)],
            dst.at[me, band, :], loc_sem.at[which],
        )

    def keep(p):
        return pltpu.make_async_copy(paired.at[p], own.at[p, me], loc_sem.at[2 + p])

    def second_too(fn):
        fn(0)
        pl.when(sec == 1)(lambda: fn(1))

    for j in range(1, n):
        second_too(lambda which: za_copy(which, j).start())
    second_too(lambda which: local(which).start())

    for p in range(pieces):
        for which in (0, 1):
            weight_copy(which, p).wait()
            rows_in = (normed, second)[which]
            paired[p, :, which * half : (which + 1) * half] = jnp.dot(
                rows_in[...], wbuf[which, p], preferred_element_type=jnp.float32
            ).astype(jnp.bfloat16)
        for way in (0, 1):
            pl.when(line_ok(way, 0))(lambda way=way, p=p: line_copy(way, 0, p).start())
        sec_copy(me, p, paired.at[p]).start()
        keep(p).start()

    def spread(which):
        local(which).wait()
        for j in range(1, n):
            za_copy(which, j).wait_recv()
        for j in range(1, m):
            mp_copy(which, j).start()

    second_too(spread)

    for wave in range(pieces + n - 2):
        for s in range(max(0, wave - pieces + 1), min(n - 1, wave + 1)):
            p = wave - s
            for way in (0, 1):

                @pl.when(got(way, s))
                def _():
                    line_copy(way, s, p).wait_recv()
                    chunk = me - 1 - s if way == 0 else me + 1 + s
                    if s + 1 < n - 1:
                        pl.when(line_ok(way, s + 1))(
                            lambda: line_copy(way, s + 1, p).start()
                        )
                    sec_copy(chunk, p, own.at[p, chunk]).start()

        p = wave - (n - 2)
        if p >= 0:
            keep(p).wait()
            for c in range(n):
                sec_copy(c, p, own.at[p, c]).wait_recv()
            attend_piece(
                sec == 0, p, group, id_col, id_row, own, other, out_a, out_b, acc_a, acc_b
            )

    def finish(which):
        for j in range(1, n):
            za_copy(which, j).wait_send()
        for j in range(1, m):
            mp_copy(which, j).wait()

    second_too(finish)
    for p in range(pieces):
        for s in range(n - 1):
            for way in (0, 1):
                pl.when(line_ok(way, s))(
                    lambda way=way, s=s, p=p: line_copy(way, s, p).wait_send()
                )
        for c in range(n):
            sec_copy(c, p, own.at[p, c]).wait_send()


def forward(n, m, normed, second, id_c, id_r, proj_a, proj_b):
    tokens, width = normed.shape
    inner = proj_a.shape[2]
    half = 2 * LANES
    pieces = inner // half
    rows = n * tokens
    group = max(1, min(n, 512 * 512 // (rows * tokens)))
    blocks = n // group
    grad = jax.ShapeDtypeStruct((n, tokens, inner), jnp.bfloat16)
    mine = jax.ShapeDtypeStruct((n, tokens, width // n), jnp.bfloat16)
    acc = (rows, LANES) if blocks > 1 else (8, LANES)
    dma = pltpu.SemaphoreType.DMA
    vmem = pl.BlockSpec(memory_space=pltpu.VMEM)
    anyw = pl.BlockSpec(memory_space=pltpu.HBM)
    bf16 = jnp.bfloat16
    return pl.pallas_call(
        functools.partial(forward_kernel, n, m, group),
        out_shape=(grad, grad, mine, mine),
        in_specs=[vmem] * 4 + [anyw] * 2,
        out_specs=[vmem, vmem, anyw, anyw],
        scratch_shapes=[
            pltpu.VMEM((2, pieces, width, half), bf16),
            pltpu.VMEM((pieces, tokens, 2 * half), bf16),
            pltpu.VMEM((pieces, n, tokens, 2 * half), bf16),
            pltpu.VMEM((pieces, n, tokens, 2 * half), bf16),
            pltpu.VMEM(acc, jnp.float32), pltpu.VMEM(acc, jnp.float32),
            dma((2, pieces)),
            dma((2, n, pieces)), dma((2, n, pieces)), dma((n, pieces)), dma((n, pieces)),
            dma((2, n)), dma((2, n)), dma((2, m)), dma((2, m)), dma((2 + pieces,)),
        ],
        compiler_params=pltpu.CompilerParams(
            collective_id=0, has_side_effects=True, vmem_limit_bytes=67000000
        ),
        name="forward",
    )(normed, second, id_c.reshape(n, tokens, 1), id_r.reshape(blocks, 1, rows // blocks),
      proj_a, proj_b)


def reduce_kernel(
    m, grad_a, grad_b, proj_a, proj_b, x_ref, gain_ref, result,
    left, wbuf, total, mine, partial, landed, gsem, wsem, send, recv,
):
    me = lax.axis_index("dp")
    col = lax.axis_index("mp")
    encoder = lax.axis_index("section") == 0
    tokens = x_ref.shape[0]
    part = tokens // m
    chunks, step = wbuf.shape[1:3]

    def left_copy(which):
        return pltpu.make_async_copy(
            (grad_a, grad_b)[which].at[me], left.at[which], gsem.at[which]
        )

    def weight_copy(which, c):
        return pltpu.make_async_copy(
            (proj_a, proj_b)[which].at[0, pl.ds(c * step, step), :],
            wbuf.at[which, c], wsem.at[which, c],
        )

    left_copy(0).start()
    pl.when(encoder)(lambda: left_copy(1).start())
    for c in range(chunks):
        weight_copy(0, c).start()
        pl.when(encoder)(lambda c=c: weight_copy(1, c).start())

    barrier = pltpu.get_barrier_semaphore()
    for j in range(1, m):
        pl.semaphore_signal(
            barrier, inc=1, device_id={"mp": lax.rem(col + j, m)}, device_id_type=MESH
        )
    pl.semaphore_wait(barrier, m - 1)

    def scatter(j, c):
        peer = lax.rem(col + j, m)
        rows = pl.ds(pl.multiple_of(peer * part, part), part)
        at = pl.ds(c * step, step)
        return pltpu.make_async_remote_copy(
            src_ref=partial.at[rows, at], dst_ref=landed.at[j, :, at],
            send_sem=send.at[j, c], recv_sem=recv.at[j, c],
            device_id={"mp": peer}, device_id_type=MESH,
        )

    band = pl.ds(pl.multiple_of(col * part, part), part)
    left_copy(0).wait()
    pl.when(encoder)(lambda: left_copy(1).wait())
    for c in range(chunks):
        weight_copy(0, c).wait()
        total[...] = right_product(left[0], wbuf[0, c])

        @pl.when(encoder)
        def _():
            weight_copy(1, c).wait()
            total[...] += right_product(left[1], wbuf[1, c])

        partial[:, c * step : (c + 1) * step] = total[...].astype(jnp.bfloat16)
        mine[:, c * step : (c + 1) * step] = total[band, :]
        for j in range(1, m):
            scatter(j, c).start()
    x = x_ref[band, :].astype(jnp.float32)
    scale = lax.rsqrt(jnp.mean(x * x, axis=-1, keepdims=True) + EPS)
    for j in range(1, m):
        for c in range(chunks):
            scatter(j, c).wait_recv()
    dnorm = mine[...]
    for j in range(1, m):
        dnorm = dnorm + landed[j].astype(jnp.float32)
    upper = gain_ref[...] * dnorm
    inner = jnp.mean(x * upper, axis=-1, keepdims=True)
    result[...] = (scale * upper - x * scale * scale * scale * inner).astype(jnp.bfloat16)
    for j in range(1, m):
        for c in range(chunks):
            scatter(j, c).wait_send()


def reduce_norm(m, grad_a, grad_b, proj_a, proj_b, states, gain):
    tokens, width = states.shape
    inner = proj_a.shape[2]
    part = tokens // m
    step = 4 * LANES
    chunks = width // step
    dma = pltpu.SemaphoreType.DMA
    bf16, f32 = jnp.bfloat16, jnp.float32
    vmem = pl.BlockSpec(memory_space=pltpu.VMEM)
    return pl.pallas_call(
        functools.partial(reduce_kernel, m),
        out_shape=jax.ShapeDtypeStruct((part, width), bf16),
        in_specs=[pl.BlockSpec(memory_space=pltpu.HBM)] * 4 + [vmem] * 2,
        out_specs=vmem,
        scratch_shapes=[
            pltpu.VMEM((2, tokens, inner), bf16),
            pltpu.VMEM((2, chunks, step, inner), bf16),
            pltpu.VMEM((tokens, step), f32),
            pltpu.VMEM((part, width), f32),
            pltpu.VMEM((tokens, width), bf16),
            pltpu.VMEM((m, part, width), bf16),
            dma((2,)), dma((2, chunks)), dma((m, chunks)), dma((m, chunks)),
        ],
        compiler_params=pltpu.CompilerParams(
            collective_id=1, has_side_effects=True, vmem_limit_bytes=66500000
        ),
        name="reduce_norm",
    )(grad_a, grad_b, proj_a, proj_b, states, gain)


def per_device(states, gains, proj_a, proj_b, cotangent, src_len, tgt_len, dest):
    encoder = lax.axis_index("section") == 0
    member = lax.axis_index("dp")
    n = lax.axis_size("dp")
    m = lax.axis_size("mp")
    gain = gains[0]
    weight_a = proj_a[0]
    weight_b = proj_b[0]
    tokens = states.shape[1]
    _, _, normed = rms_forward(states[0], gain)
    second_left = jnp.where(encoder, normed, cotangent)
    rows = n * tokens
    seqs = tgt_len.shape[1]
    names = jnp.arange(n * seqs, dtype=jnp.int32).reshape(n, seqs)
    qid = sequence_of(tgt_len, names, tokens)
    kid = sequence_of(src_len, dest, tokens)
    grad_first, grad_second, mine_a, mine_b = forward(
        n, m, normed, second_left, jnp.where(encoder, kid, qid), jnp.where(encoder, qid, kid),
        proj_a, proj_b,
    )
    mine = reduce_norm(m, grad_first, grad_second, proj_a, proj_b, states[0], gains)
    col = lax.axis_index("mp")
    landed = [mine] + [
        lax.ppermute(mine, "mp", [(i, (i + j) % m) for i in range(m)]) for j in range(1, m)
    ]
    mine_a = mine_a.reshape(rows, -1)
    mine_b = jnp.where(encoder, mine_a, mine_b.reshape(rows, -1))
    grad_a = left_product(mine_a, grad_first.reshape(rows, -1))
    grad_b = left_product(mine_b, grad_second.reshape(rows, -1))
    bands = []
    for b in range(m):
        band = landed[0]
        for j in range(1, m):
            band = jnp.where(col == (b + j) % m, landed[j], band)
        bands.append(band)
    grad_states = jnp.concatenate(bands, axis=0)
    return (grad_states[None], grad_a[None], grad_b[None])


def solution(mesh):
    return jax.shard_map(
        per_device,
        mesh=mesh,
        in_specs=(
            P("section", "dp", None),
            P("section", None),
            P("section", None, "mp"),
            P("section", None, "mp"),
            P("dp", None),
            P(),
            P(),
            P(),
        ),
        out_specs=(P("section", "dp", None), P("section", "dp", "mp"), P("section", "dp", "mp")),
        check_vma=False,
    )
```

```python
import functools

import jax
import jax.numpy as jnp
from jax import lax
from jax.experimental import pallas as pl
from jax.experimental.pallas import tpu as pltpu
from jax.sharding import PartitionSpec as P

HEAD_DIM = 64
LANES = 128
EPS = 1e-06
MESH = pl.DeviceIdType.MESH


def rms_forward(states_row, gain):
    xf = states_row.astype(jnp.float32)
    scale = lax.rsqrt(jnp.mean(xf * xf, axis=-1, keepdims=True) + EPS)
    return (xf, scale, (xf * scale * gain).astype(jnp.bfloat16))


def left_product(left, right):
    return lax.dot_general(
        left, right, (((0,), (0,)), ((), ())), preferred_element_type=jnp.float32
    )


def right_product(rows, weight):
    return lax.dot_general(
        rows, weight, (((1,), (1,)), ((), ())), preferred_element_type=jnp.float32
    )


def sequence_of(lengths, names, tokens):
    slot = jnp.arange(lengths.shape[1], dtype=jnp.int32)
    before = slot[:, None] < slot[None, :]
    starts = jnp.sum(jnp.where(before[None], lengths[:, :, None], 0), axis=1)
    place = jnp.arange(tokens, dtype=jnp.int32)[None, :, None]
    offset = place - starts[:, None, :]
    inside = (offset >= 0) & (offset < lengths[:, None, :])
    return jnp.sum(jnp.where(inside, names[:, None, :], 0), axis=-1).reshape(-1)


def attend_piece(encoder, p, group, id_col, id_row, own, other, out_a, out_b, acc_a, acc_b):
    n, tokens, width = own.shape[1:]
    half = width // 2
    rows = n * tokens
    blocks = n // group
    lane = lax.broadcasted_iota(jnp.int32, (1, LANES), 1) // HEAD_DIM
    zero = jnp.zeros((), jnp.bfloat16)
    f32 = jnp.float32

    def cut(ref, which, c, at):
        lo = pl.multiple_of(which * half + c * LANES, LANES)
        return ref[p, at, :, pl.ds(lo, LANES)].reshape(-1, LANES)

    every = pl.ds(0, n)

    @pl.loop(0, half // LANES)
    def _(c):
        out_cols = pl.ds(pl.multiple_of(p * half + c * LANES, LANES), LANES)

        @pl.when(encoder)
        def _():
            keys, values = cut(own, 0, c, every), cut(own, 1, c, every)
            if blocks > 1:
                acc_a[...] = jnp.zeros_like(acc_a)
                acc_b[...] = jnp.zeros_like(acc_b)

            def block(b):
                at = pl.ds(b * group, group)
                query, dout = cut(other, 0, c, at), cut(other, 1, c, at)
                mask = id_col[...].reshape(rows, 1) == id_row[b]
                dk, dv = None, None
                for h in range(LANES // HEAD_DIM):
                    qh = jnp.where(lane == h, query, zero)
                    dh = jnp.where(lane == h, dout, zero)
                    expo = jnp.exp(jnp.where(mask, right_product(keys, qh), -jnp.inf))
                    weight = expo * (1.0 / jnp.sum(expo, axis=0, keepdims=True))
                    dweight = right_product(values, dh)
                    total = jnp.sum(weight * dweight, axis=0, keepdims=True)
                    dscore = (weight * (dweight - total)).astype(jnp.bfloat16)
                    pk = jnp.dot(dscore, qh, preferred_element_type=f32)
                    pv = jnp.dot(weight.astype(jnp.bfloat16), dh, preferred_element_type=f32)
                    dk = pk if dk is None else dk + pk
                    dv = pv if dv is None else dv + pv
                if blocks == 1:
                    out_a[:, :, out_cols] = dk.astype(jnp.bfloat16).reshape(n, tokens, LANES)
                    out_b[:, :, out_cols] = dv.astype(jnp.bfloat16).reshape(n, tokens, LANES)
                else:
                    acc_a[...] += dk
                    acc_b[...] += dv

            if blocks == 1:
                block(0)
            else:
                pl.loop(0, blocks)(block)
                out_a[:, :, out_cols] = acc_a[...].astype(jnp.bfloat16).reshape(n, tokens, LANES)
                out_b[:, :, out_cols] = acc_b[...].astype(jnp.bfloat16).reshape(n, tokens, LANES)

        @pl.when(jnp.logical_not(encoder))
        def _():
            keys, values = cut(other, 0, c, every), cut(other, 1, c, every)

            def block(b):
                at = pl.ds(b * group, group)
                query, dout = cut(own, 0, c, at), cut(own, 1, c, at)
                ids = id_col[at, :, :].reshape(group * tokens, 1)
                mask = None
                dq, att = None, None
                for h in range(LANES // HEAD_DIM):
                    kh = jnp.where(lane == h, keys, zero)
                    vh = jnp.where(lane == h, values, zero)
                    score = right_product(query, kh)
                    if mask is None:
                        span = group * tokens
                        mask = jnp.concatenate(
                            [ids == id_row[i] for i in range(rows // span)], axis=1
                        )
                    expo = jnp.exp(jnp.where(mask, score, -jnp.inf))
                    weight = expo * (1.0 / jnp.sum(expo, axis=1, keepdims=True))
                    dweight = right_product(dout, vh)
                    total = jnp.sum(weight * dweight, axis=1, keepdims=True)
                    dscore = (weight * (dweight - total)).astype(jnp.bfloat16)
                    pq = jnp.dot(dscore, kh, preferred_element_type=f32)
                    pa = jnp.dot(weight.astype(jnp.bfloat16), vh, preferred_element_type=f32)
                    dq = pq if dq is None else dq + pq
                    att = pa if att is None else att + pa
                shape = (group, tokens, LANES)
                out_a[at, :, out_cols] = dq.astype(jnp.bfloat16).reshape(shape)
                out_b[at, :, out_cols] = att.astype(jnp.bfloat16).reshape(shape)

            if blocks == 1:
                block(0)
            else:
                pl.loop(0, blocks)(block)


def forward_kernel(
    n, m, group, normed, second, id_col, id_row, proj_a, proj_b,
    out_a, out_b, mine_a, mine_b,
    wbuf, paired, own, other, acc_a, acc_b, wsem,
    line_send, line_recv, sec_send, sec_recv, za_send, za_recv, mp_send, mp_recv, loc_sem,
):
    me = lax.axis_index("dp")
    col = lax.axis_index("mp")
    sec = lax.axis_index("section")
    tokens, width = normed.shape
    pieces = wbuf.shape[1]
    half = wbuf.shape[3]
    part = tokens // m
    cols = width // n

    def weight_copy(which, p):
        src = (proj_a, proj_b)[which]
        return pltpu.make_async_copy(
            src.at[0, :, pl.ds(p * half, half)], wbuf.at[which, p], wsem.at[which, p]
        )

    for p in range(pieces):
        for which in (0, 1):
            weight_copy(which, p).start()

    barrier = pltpu.get_barrier_semaphore()
    for j in range(1, n):
        pl.semaphore_signal(
            barrier, inc=1, device_id={"dp": lax.rem(me + j, n)}, device_id_type=MESH
        )
    for j in range(1, m):
        pl.semaphore_signal(
            barrier, inc=1, device_id={"mp": lax.rem(col + j, m)}, device_id_type=MESH
        )
    pl.semaphore_signal(barrier, inc=1, device_id={"section": 1 - sec}, device_id_type=MESH)
    pl.semaphore_wait(barrier, n + m - 1)

    band = pl.ds(pl.multiple_of(col * part, part), part)

    def line_copy(way, s, p):
        chunk = me - s if way == 0 else me + s
        target = me + 1 if way == 0 else me - 1
        src = paired.at[p] if s == 0 else own.at[p, chunk]
        return pltpu.make_async_remote_copy(
            src_ref=src, dst_ref=own.at[p, chunk],
            send_sem=line_send.at[way, s, p], recv_sem=line_recv.at[way, s, p],
            device_id={"dp": target}, device_id_type=MESH,
        )

    def line_ok(way, s):
        if way == 0:
            return jnp.logical_and(me - s >= 0, me < n - 1)
        return jnp.logical_and(me + s <= n - 1, me > 0)

    def got(way, s):
        return me - 1 - s >= 0 if way == 0 else me + 1 + s <= n - 1

    def sec_copy(chunk, p, src):
        return pltpu.make_async_remote_copy(
            src_ref=src, dst_ref=other.at[p, chunk],
            send_sem=sec_send.at[chunk, p], recv_sem=sec_recv.at[chunk, p],
            device_id={"section": 1 - sec}, device_id_type=MESH,
        )

    def za_copy(which, j):
        src, dst = ((normed, mine_a), (second, mine_b))[which]
        peer = lax.rem(me + j, n)
        return pltpu.make_async_remote_copy(
            src_ref=src.at[band, pl.ds(pl.multiple_of(peer * cols, cols), cols)],
            dst_ref=dst.at[me, band, :],
            send_sem=za_send.at[which, j], recv_sem=za_recv.at[which, j],
            device_id={"dp": peer}, device_id_type=MESH,
        )

    def mp_copy(which, j):
        dst = (mine_a, mine_b)[which]
        return pltpu.make_async_remote_copy(
            src_ref=dst.at[:, band, :], dst_ref=dst.at[:, band, :],
            send_sem=mp_send.at[which, j], recv_sem=mp_recv.at[which, j],
            device_id={"mp": lax.rem(col + j, m)}, device_id_type=MESH,
        )

    def local(which):
        src, dst = ((normed, mine_a), (second, mine_b))[which]
        return pltpu.make_async_copy(
            src.at[band, pl.ds(pl.multiple_of(me * cols, cols), cols)],
            dst.at[me, band, :], loc_sem.at[which],
        )

    def keep(p):
        return pltpu.make_async_copy(paired.at[p], own.at[p, me], loc_sem.at[2 + p])

    def second_too(fn):
        fn(0)
        pl.when(sec == 1)(lambda: fn(1))

    for j in range(1, n):
        second_too(lambda which: za_copy(which, j).start())
    second_too(lambda which: local(which).start())

    for p in range(pieces):
        for which in (0, 1):
            weight_copy(which, p).wait()
            rows_in = (normed, second)[which]
            paired[p, :, which * half : (which + 1) * half] = jnp.dot(
                rows_in[...], wbuf[which, p], preferred_element_type=jnp.float32
            ).astype(jnp.bfloat16)
        for way in (0, 1):
            pl.when(line_ok(way, 0))(lambda way=way, p=p: line_copy(way, 0, p).start())
        sec_copy(me, p, paired.at[p]).start()
        keep(p).start()

    def spread(which):
        local(which).wait()
        for j in range(1, n):
            za_copy(which, j).wait_recv()
        for j in range(1, m):
            mp_copy(which, j).start()

    second_too(spread)

    for wave in range(pieces + n - 2):
        for s in range(max(0, wave - pieces + 1), min(n - 1, wave + 1)):
            p = wave - s
            for way in (0, 1):

                @pl.when(got(way, s))
                def _():
                    line_copy(way, s, p).wait_recv()
                    chunk = me - 1 - s if way == 0 else me + 1 + s
                    if s + 1 < n - 1:
                        pl.when(line_ok(way, s + 1))(
                            lambda: line_copy(way, s + 1, p).start()
                        )
                    sec_copy(chunk, p, own.at[p, chunk]).start()

        p = wave - (n - 2)
        if p >= 0:
            keep(p).wait()
            for c in range(n):
                sec_copy(c, p, own.at[p, c]).wait_recv()
            attend_piece(
                sec == 0, p, group, id_col, id_row, own, other, out_a, out_b, acc_a, acc_b
            )

    def finish(which):
        for j in range(1, n):
            za_copy(which, j).wait_send()
        for j in range(1, m):
            mp_copy(which, j).wait()

    second_too(finish)
    for p in range(pieces):
        for s in range(n - 1):
            for way in (0, 1):
                pl.when(line_ok(way, s))(
                    lambda way=way, s=s, p=p: line_copy(way, s, p).wait_send()
                )
        for c in range(n):
            sec_copy(c, p, own.at[p, c]).wait_send()


def forward(n, m, normed, second, id_c, id_r, proj_a, proj_b):
    tokens, width = normed.shape
    inner = proj_a.shape[2]
    half = 2 * LANES
    pieces = inner // half
    rows = n * tokens
    group = max(1, min(n, 512 * 512 // (rows * tokens)))
    blocks = n // group
    grad = jax.ShapeDtypeStruct((n, tokens, inner), jnp.bfloat16)
    mine = jax.ShapeDtypeStruct((n, tokens, width // n), jnp.bfloat16)
    acc = (rows, LANES) if blocks > 1 else (8, LANES)
    dma = pltpu.SemaphoreType.DMA
    vmem = pl.BlockSpec(memory_space=pltpu.VMEM)
    anyw = pl.BlockSpec(memory_space=pltpu.HBM)
    bf16 = jnp.bfloat16
    return pl.pallas_call(
        functools.partial(forward_kernel, n, m, group),
        out_shape=(grad, grad, mine, mine),
        in_specs=[vmem] * 4 + [anyw] * 2,
        out_specs=[vmem, vmem, anyw, anyw],
        scratch_shapes=[
            pltpu.VMEM((2, pieces, width, half), bf16),
            pltpu.VMEM((pieces, tokens, 2 * half), bf16),
            pltpu.VMEM((pieces, n, tokens, 2 * half), bf16),
            pltpu.VMEM((pieces, n, tokens, 2 * half), bf16),
            pltpu.VMEM(acc, jnp.float32), pltpu.VMEM(acc, jnp.float32),
            dma((2, pieces)),
            dma((2, n, pieces)), dma((2, n, pieces)), dma((n, pieces)), dma((n, pieces)),
            dma((2, n)), dma((2, n)), dma((2, m)), dma((2, m)), dma((2 + pieces,)),
        ],
        compiler_params=pltpu.CompilerParams(
            collective_id=0, has_side_effects=True, vmem_limit_bytes=67000000
        ),
        name="forward",
    )(normed, second, id_c.reshape(n, tokens, 1), id_r.reshape(blocks, 1, rows // blocks),
      proj_a, proj_b)


def reduce_kernel(
    m, grad_a, grad_b, proj_a, proj_b, x_ref, gain_ref, result,
    left, wbuf, total, mine, partial, landed, gsem, wsem, send, recv,
):
    me = lax.axis_index("dp")
    col = lax.axis_index("mp")
    encoder = lax.axis_index("section") == 0
    tokens = x_ref.shape[0]
    part = tokens // m
    chunks, step = wbuf.shape[1:3]

    def left_copy(which):
        return pltpu.make_async_copy(
            (grad_a, grad_b)[which].at[me], left.at[which], gsem.at[which]
        )

    def weight_copy(which, c):
        return pltpu.make_async_copy(
            (proj_a, proj_b)[which].at[0, pl.ds(c * step, step), :],
            wbuf.at[which, c], wsem.at[which, c],
        )

    left_copy(0).start()
    pl.when(encoder)(lambda: left_copy(1).start())
    for c in range(chunks):
        weight_copy(0, c).start()
        pl.when(encoder)(lambda c=c: weight_copy(1, c).start())

    barrier = pltpu.get_barrier_semaphore()
    for j in range(1, m):
        pl.semaphore_signal(
            barrier, inc=1, device_id={"mp": lax.rem(col + j, m)}, device_id_type=MESH
        )
    pl.semaphore_wait(barrier, m - 1)

    def scatter(j, c):
        peer = lax.rem(col + j, m)
        rows = pl.ds(pl.multiple_of(peer * part, part), part)
        at = pl.ds(c * step, step)
        return pltpu.make_async_remote_copy(
            src_ref=partial.at[rows, at], dst_ref=landed.at[j, :, at],
            send_sem=send.at[j, c], recv_sem=recv.at[j, c],
            device_id={"mp": peer}, device_id_type=MESH,
        )

    band = pl.ds(pl.multiple_of(col * part, part), part)
    left_copy(0).wait()
    pl.when(encoder)(lambda: left_copy(1).wait())
    for c in range(chunks):
        weight_copy(0, c).wait()
        total[...] = right_product(left[0], wbuf[0, c])

        @pl.when(encoder)
        def _():
            weight_copy(1, c).wait()
            total[...] += right_product(left[1], wbuf[1, c])

        partial[:, c * step : (c + 1) * step] = total[...].astype(jnp.bfloat16)
        mine[:, c * step : (c + 1) * step] = total[band, :]
        for j in range(1, m):
            scatter(j, c).start()
    x = x_ref[band, :].astype(jnp.float32)
    scale = lax.rsqrt(jnp.mean(x * x, axis=-1, keepdims=True) + EPS)
    for j in range(1, m):
        for c in range(chunks):
            scatter(j, c).wait_recv()
    dnorm = mine[...]
    for j in range(1, m):
        dnorm = dnorm + landed[j].astype(jnp.float32)
    upper = gain_ref[...] * dnorm
    inner = jnp.mean(x * upper, axis=-1, keepdims=True)
    result[...] = (scale * upper - x * scale * scale * scale * inner).astype(jnp.bfloat16)
    for j in range(1, m):
        for c in range(chunks):
            scatter(j, c).wait_send()


def reduce_norm(m, grad_a, grad_b, proj_a, proj_b, states, gain):
    tokens, width = states.shape
    inner = proj_a.shape[2]
    part = tokens // m
    step = 4 * LANES
    chunks = width // step
    dma = pltpu.SemaphoreType.DMA
    bf16, f32 = jnp.bfloat16, jnp.float32
    vmem = pl.BlockSpec(memory_space=pltpu.VMEM)
    return pl.pallas_call(
        functools.partial(reduce_kernel, m),
        out_shape=jax.ShapeDtypeStruct((part, width), bf16),
        in_specs=[pl.BlockSpec(memory_space=pltpu.HBM)] * 4 + [vmem] * 2,
        out_specs=vmem,
        scratch_shapes=[
            pltpu.VMEM((2, tokens, inner), bf16),
            pltpu.VMEM((2, chunks, step, inner), bf16),
            pltpu.VMEM((tokens, step), f32),
            pltpu.VMEM((part, width), f32),
            pltpu.VMEM((tokens, width), bf16),
            pltpu.VMEM((m, part, width), bf16),
            dma((2,)), dma((2, chunks)), dma((m, chunks)), dma((m, chunks)),
        ],
        compiler_params=pltpu.CompilerParams(
            collective_id=1, has_side_effects=True, vmem_limit_bytes=66500000
        ),
        name="reduce_norm",
    )(grad_a, grad_b, proj_a, proj_b, states, gain)


def per_device(states, gains, proj_a, proj_b, cotangent, src_len, tgt_len, dest):
    encoder = lax.axis_index("section") == 0
    member = lax.axis_index("dp")
    n = lax.axis_size("dp")
    m = lax.axis_size("mp")
    gain = gains[0]
    weight_a = proj_a[0]
    weight_b = proj_b[0]
    tokens = states.shape[1]
    _, _, normed = rms_forward(states[0], gain)
    second_left = jnp.where(encoder, normed, cotangent)
    rows = n * tokens
    seqs = tgt_len.shape[1]
    names = jnp.arange(n * seqs, dtype=jnp.int32).reshape(n, seqs)
    id_c = sequence_of(
        jnp.where(encoder, src_len, tgt_len), jnp.where(encoder, dest, names), tokens
    )
    id_r = sequence_of(
        jnp.where(encoder, tgt_len, src_len), jnp.where(encoder, names, dest), tokens
    )
    grad_first, grad_second, mine_a, mine_b = forward(
        n, m, normed, second_left, id_c, id_r, proj_a, proj_b
    )
    mine = reduce_norm(m, grad_first, grad_second, proj_a, proj_b, states[0], gains)
    col = lax.axis_index("mp")
    landed = [mine] + [
        lax.ppermute(mine, "mp", [(i, (i + j) % m) for i in range(m)]) for j in range(1, m)
    ]
    mine_a = mine_a.reshape(rows, -1)
    mine_b = jnp.where(encoder, mine_a, mine_b.reshape(rows, -1))
    grad_a = left_product(mine_a, grad_first.reshape(rows, -1))
    grad_b = left_product(mine_b, grad_second.reshape(rows, -1))
    bands = []
    for b in range(m):
        band = landed[0]
        for j in range(1, m):
            band = jnp.where(col == (b + j) % m, landed[j], band)
        bands.append(band)
    grad_states = jnp.concatenate(bands, axis=0)
    return (grad_states[None], grad_a[None], grad_b[None])


def solution(mesh):
    return jax.shard_map(
        per_device,
        mesh=mesh,
        in_specs=(
            P("section", "dp", None),
            P("section", None),
            P("section", None, "mp"),
            P("section", None, "mp"),
            P("dp", None),
            P(),
            P(),
            P(),
        ),
        out_specs=(P("section", "dp", None), P("section", "dp", "mp"), P("section", "dp", "mp")),
        check_vma=False,
    )
```
